32 devices in a mesh: worker: 8 (over z, y), mp: 4 (over x, core).
Axes of the slice: x: 2, y: 2, z: 4, core: 2. Of those that a mesh axis runs over, the one named last changes fastest.
Arguments:
- gradients: bfloat16 [128, 1048576], P('worker', 'mp'), may hold values from -30 to 30
- center: float32 [1048576], P('mp'), may hold values from -6 to 6
- outside_sq: float32 [3, 128], P(None, 'worker'), may hold values from 209715.2 to 2097152
- radius: float32 [3], replicated, may hold values from 1.5 to 3
Outputs:
- new_center: float32 [1048576], P('mp')
- norms: float32 [128], P('worker')
The draws below stay inside these ranges and needn't reach their ends.
All inputs are finite; a program needn't handle non-finite values.
Results may differ from the reference program's by a relative error of at most 0.0003.
Values sent between devices are 32-bit elements; how exact they have to be, the bound alone decides.
No kernel may reach another device: no remote copies, remote signals or barrier semaphores. Data moves between devices by JAX's collectives and lax.ppermute only.
A program may use at most 64 MiB of HBM per device.

```python
import math
import jax
import jax.numpy as jnp
from jax import lax

W_DEV = 16
ITERS = 3
WORKERS = 128
P_SIZE = 1048576


def draw_gradients(key, part):
    first = jax.random.fold_in(key, 11)
    second = jax.random.fold_in(key, 12)
    scales = jnp.exp(jax.random.uniform(first, (WORKERS, 1), jnp.float32, jnp.log(0.3), jnp.log(5.0)))
    values = scales * jnp.clip(jax.random.normal(second, (WORKERS, P_SIZE), jnp.float32), -6.0, 6.0)
    return values.astype(jnp.bfloat16)


def block_scale(rng, extent, shards, smallest, high):
    loudness = 1.0
    for dim, shards_of in shards:
        draws = jax.random.uniform(jax.random.fold_in(jax.random.fold_in(rng, 6), dim), (shards_of,), jnp.float32, smallest / len(shards), high / len(shards))
        loudness = loudness * jnp.repeat(jnp.exp(draws), extent[dim] // shards_of).reshape((-1,) + (1,) * (len(extent) - 1 - dim))
    return loudness


def gaussian(stream_key, dims, width, reach, cuts=(), kind=jnp.bfloat16):
    entries = jax.random.normal(stream_key, dims, jnp.float32) * width
    if len(cuts) > 0:
        entries = block_scale(stream_key, dims, cuts, -0.22, 0.18) * entries
    return jnp.clip(entries, min=-reach, max=reach).astype(kind)


def setup_inputs(seed: int = 0) -> dict:
    seeds = jax.random.split(jax.random.key(seed), 5)
    gradients = draw_gradients(jax.random.fold_in(seeds[4], 71), 0)
    center = gaussian(seeds[1], (P_SIZE,), 1.0, 6.0, ((0, 4),), jnp.float32)
    outside_sq = jnp.clip(209715.2 + 1887436.8 * jax.random.uniform(seeds[2], (ITERS, WORKERS), jnp.float32) ** block_scale(seeds[2], (ITERS, WORKERS), ((1, 8),), -0.2, 0.2), 209715.2, 2097152)
    radius = jnp.clip(jnp.exp(jax.random.uniform(seeds[3], (ITERS,), jnp.float32, math.log(1.5), math.log(3.0))), 1.5, 3.0)
    return dict(gradients=gradients, center=center, outside_sq=outside_sq, radius=radius)


def reference(gradients, center, outside_sq, radius):
    blocks = gradients.reshape(WORKERS // W_DEV, W_DEV, P_SIZE)
    root_total = jnp.sqrt(jnp.float32(P_SIZE))
    value = center
    norms = jnp.zeros((WORKERS,), jnp.float32)
    for step in range(ITERS):

        def squares(block):
            diff = block.astype(jnp.float32) - value[None, :]
            return lax.optimization_barrier(jnp.sum(diff * diff, axis=1))
        partial_value = lax.map(squares, blocks).reshape(WORKERS)
        norms = jnp.sqrt(partial_value + outside_sq[step])
        factor = jnp.minimum(jnp.float32(1.0), radius[step] * root_total / norms)
        factor_blocks = factor.reshape(WORKERS // W_DEV, W_DEV)

        def accumulate(total, pair):
            block, weights = pair
            diff = block.astype(jnp.float32) - value[None, :]
            return (total + lax.optimization_barrier(jnp.sum(weights[:, None] * diff, axis=0)), None)
        summed, unused = lax.scan(accumulate, jnp.zeros((P_SIZE,), jnp.float32), (blocks, factor_blocks))
        value = value + summed / jnp.float32(WORKERS)
    return (value, norms)
```

```python
import functools

import jax
import jax.numpy as jnp
from jax import lax
from jax.experimental import pallas as pl
from jax.experimental.pallas import tpu as pltpu
from jax.sharding import PartitionSpec as P

LANES = 128
GROUP = 8
BLOCK = 32
VMEM_LIMIT = 24 << 20


def bits_of(size):
    count = size.bit_length() - 1
    assert 1 << count == size
    return count


def swap(size, bit):
    return [(i, i ^ (1 << bit)) for i in range(size)]


def square_rows(x_ref, x_row, v_ref, v_row, rows, carry, limit):
    unroll = 16

    def step(i, acc):
        acc = list(acc)
        for r in range(0, unroll, 2):
            row = v_row + i * unroll + r
            first = v_ref[pl.ds(row, 1), :]
            second = v_ref[pl.ds(row + 1, 1), :]
            at = (x_row + i * unroll + r) * GROUP
            for g in range(len(acc) // 2):
                both = x_ref[g, pl.ds(pl.multiple_of(at, 2 * GROUP), 2 * GROUP), :].astype(jnp.float32)
                a = both[:GROUP] - first
                b = both[GROUP:] - second
                acc[2 * g] = acc[2 * g] + a * a
                acc[2 * g + 1] = acc[2 * g + 1] + b * b
        return tuple(acc)

    return lax.fori_loop(0, rows // unroll, step, carry)


def zero_carry(groups):
    return tuple(jnp.zeros((GROUP, LANES), jnp.float32) for _ in range(2 * groups))


def store_carry(o_ref, acc):
    for g in range(len(acc) // 2):
        o_ref[pl.ds(g * GROUP, GROUP), :] = acc[2 * g] + acc[2 * g + 1]


def load_body(chunks, x_hbm, v_ref, x_ref, o_ref, sems):
    groups, total, _ = x_ref.shape
    rows = total // chunks

    def copy(c):
        window = pl.ds(pl.multiple_of(c * rows, 2 * GROUP), rows)
        return pltpu.make_async_copy(x_hbm.at[:, window, :], x_ref.at[:, window, :], sems.at[c])

    for c in range(chunks):
        copy(c).start()
    acc = zero_carry(groups)
    per = rows // GROUP
    for c in range(chunks):
        copy(c).wait()
        acc = square_rows(x_ref, c * per, v_ref, c * per, per, acc, per)
    store_carry(o_ref, acc)


def square_body(pieces, offs_ref, x_ref, v_ref, o_ref):
    groups = x_ref.shape[0]
    rows = v_ref.shape[0] // pieces
    acc = zero_carry(groups)
    for j in range(pieces):
        acc = square_rows(x_ref, pl.multiple_of(offs_ref[j], BLOCK), v_ref, j * rows, rows, acc, rows)
    store_carry(o_ref, acc)


def weigh_body(pieces, relative, devices, workers, root_total, offs_ref, radius_ref, x_ref, v_ref, s_ref, out_ref, o_ref):
    groups = x_ref.shape[0]
    rows = o_ref.shape[0] // pieces
    depth = BLOCK * GROUP
    squared = jnp.sum(s_ref[...], axis=1, keepdims=True) + out_ref[:, 0:1]
    factor = jnp.minimum(jnp.float32(1.0), radius_ref[0] * root_total / jnp.sqrt(squared))
    keep = jnp.float32(1.0 / devices) - jnp.sum(factor, axis=0, keepdims=True) / jnp.float32(workers)
    factor = factor / jnp.float32(workers)
    lane = lax.broadcasted_iota(jnp.int32, (GROUP, depth), 1)
    sub = lax.broadcasted_iota(jnp.int32, (GROUP, depth), 0)
    block = lax.broadcasted_iota(jnp.int32, (BLOCK, depth), 0)
    place = lax.broadcasted_iota(jnp.int32, (BLOCK, depth), 1)
    weights = []
    for g in range(groups):
        one = jnp.where(lane % GROUP == sub, factor[g * GROUP:(g + 1) * GROUP], 0.0)
        one = jnp.sum(one, axis=0, keepdims=True)
        full = jnp.where(place // GROUP == block, one, 0.0)
        high = full.astype(jnp.bfloat16)
        low = (full - high.astype(jnp.float32)).astype(jnp.bfloat16)
        weights.append(jnp.concatenate([high, low], axis=0))
    for j in range(pieces):
        base = pl.multiple_of(offs_ref[j], BLOCK)

        def step(i, _):
            at = base + i * 2 * BLOCK
            total = None
            for g in range(groups):
                left = x_ref[g, pl.ds(pl.multiple_of(at * GROUP, depth), depth), :]
                right = x_ref[g, pl.ds(pl.multiple_of(at * GROUP + depth, depth), depth), :]
                part = jnp.dot(weights[g], jnp.concatenate([left, right], axis=1), preferred_element_type=jnp.float32)
                total = part if total is None else total + part
            total = total[:BLOCK] + total[BLOCK:]
            v_at = (j * rows if relative else base) + i * 2 * BLOCK
            o_at = j * rows + i * 2 * BLOCK
            for h in range(2):
                old = v_ref[pl.ds(pl.multiple_of(v_at + h * BLOCK, BLOCK), BLOCK), :]
                o_ref[pl.ds(pl.multiple_of(o_at + h * BLOCK, BLOCK), BLOCK), :] = keep * old + total[:, h * LANES:(h + 1) * LANES]
            return 0

        lax.fori_loop(0, rows // (2 * BLOCK), step, 0)


VM = pl.BlockSpec(memory_space=pltpu.VMEM)
SM = pl.BlockSpec(memory_space=pltpu.SMEM)
PARAMS = pltpu.CompilerParams(vmem_limit_bytes=VMEM_LIMIT)


def shards(gradients, center, outside_sq, radius):
    workers, size = gradients.shape
    iters = outside_sq.shape[0]
    devices = lax.axis_size("worker")
    parts = lax.axis_size("mp")
    levels = bits_of(devices)
    root_total = float(size * parts) ** 0.5
    groups = workers // GROUP
    rows = size // LANES
    position = lax.axis_index("worker")
    bit = [(position >> d) & 1 for d in range(levels)]
    x = gradients.reshape(groups, GROUP, rows, LANES).transpose(0, 2, 1, 3).reshape(groups, rows * GROUP, LANES)
    center = center.reshape(rows, LANES)

    orders = [list(range(levels)), [1, 0] + list(range(2, levels))]
    height = rows // len(orders)
    count = 1 << (levels - 2)
    piece = height >> (levels - 1)

    def offsets(s, first):
        order = orders[s]
        out = []
        for j in range(count):
            off = jnp.int32(s * height) + (bit[order[0]] ^ first) * (height >> 1)
            for k in range(1, levels - 1):
                r = (j >> (levels - 2 - k)) & 1
                off = off + (bit[order[k]] ^ r) * (height >> (k + 1))
            out.append(off)
        return jnp.stack(out).astype(jnp.int32)

    offs = [[offsets(s, f) for f in range(2)] for s in range(len(orders))]
    partial_shape = jax.ShapeDtypeStruct((workers, LANES), jnp.float32)

    chunks = 16
    x, partial = pl.pallas_call(
        functools.partial(load_body, chunks),
        out_shape=(jax.ShapeDtypeStruct(x.shape, x.dtype), partial_shape),
        in_specs=[pl.BlockSpec(memory_space=pl.ANY), VM],
        out_specs=(VM, VM),
        scratch_shapes=[pltpu.SemaphoreType.DMA((chunks,))],
        compiler_params=PARAMS,
        name="load",
    )(x, center)

    def squares(s, first, value):
        return pl.pallas_call(
            functools.partial(square_body, count),
            out_shape=partial_shape, in_specs=[SM, VM, VM], out_specs=VM, compiler_params=PARAMS, name="squares",
        )(offs[s][first], x, value)

    def weigh(s, first, value, relative, step, squared):
        return pl.pallas_call(
            functools.partial(weigh_body, count, relative, devices, workers * devices, root_total),
            out_shape=jax.ShapeDtypeStruct((height >> 1, LANES), jnp.float32),
            in_specs=[SM, SM, VM, VM, VM, VM], out_specs=VM, compiler_params=PARAMS, name="weigh",
        )(offs[s][first], radius[step][None], x, value, squared, outside[step])

    def exchange(value, d):
        return lax.ppermute(value, "worker", swap(devices, d))

    outside = [jnp.broadcast_to(outside_sq[t][:, None], (workers, LANES)) for t in range(iters)]
    value = None
    for t in range(iters):
        for b in range(bits_of(parts)):
            partial = partial + lax.ppermute(partial, "mp", swap(parts, b))
        squared = partial
        hold = []
        for s in range(len(orders)):
            sent = weigh(s, 1, center if t == 0 else value[s][1], t > 0, t, squared)
            hold.append(exchange(sent, orders[s][0]))
        for s in range(len(orders)):
            hold[s] = hold[s] + weigh(s, 0, center if t == 0 else value[s][0], t > 0, t, squared)
        for k in range(1, levels - 1):
            for s in range(len(orders)):
                half = hold[s].shape[0] // 2
                hold[s] = hold[s][:half] + exchange(hold[s][half:], orders[s][k])
        for s in range(len(orders)):
            hold[s] = hold[s] + exchange(hold[s], orders[s][levels - 1])
        for k in reversed(range(1, levels - 1)):
            for s in range(len(orders)):
                hold[s] = jnp.concatenate([hold[s], exchange(hold[s], orders[s][k])], axis=0)
        value = [[hold[s], exchange(hold[s], orders[s][0])] for s in range(len(orders))]
        if t + 1 < iters:
            partial = None
            for first in range(2):
                for s in range(len(orders)):
                    one = squares(s, first, value[s][first])
                    partial = one if partial is None else partial + one

    norms = jnp.sqrt(jnp.sum(squared, axis=1) + outside_sq[iters - 1])
    final = []
    for s in range(len(orders)):
        tree = [value[s][f][j * piece:(j + 1) * piece] for f in range(2) for j in range(count)]
        for k in reversed(range(levels - 1)):
            turned = bit[orders[s][k]] == 1
            tree = [
                jnp.where(turned, jnp.concatenate([b, a]), jnp.concatenate([a, b]))
                for a, b in zip(tree[0::2], tree[1::2])
            ]
        final.append(tree[0])
    return jnp.concatenate(final).reshape(size), norms


def solution(mesh):
    placed = (P("worker", "mp"), P("mp"), P(None, "worker"), P())
    return jax.shard_map(
        shards, mesh=mesh, in_specs=placed, out_specs=(P("mp"), P("worker")), check_vma=False
    )
```

```python
import functools

import jax
import jax.numpy as jnp
from jax import lax
from jax.experimental import pallas as pl
from jax.experimental.pallas import tpu as pltpu
from jax.sharding import PartitionSpec as P

LANES = 128
GROUP = 8
BLOCK = 32
VMEM_LIMIT = 24 << 20


def bits_of(size):
    count = size.bit_length() - 1
    assert 1 << count == size
    return count


def swap(size, bit):
    return [(i, i ^ (1 << bit)) for i in range(size)]


def square_rows(x_ref, x_row, v_ref, v_row, rows, carry, limit):
    unroll = 16

    def step(i, acc):
        acc = list(acc)
        for r in range(0, unroll, 2):
            row = v_row + i * unroll + r
            first = v_ref[pl.ds(row, 1), :]
            second = v_ref[pl.ds(row + 1, 1), :]
            at = (x_row + i * unroll + r) * GROUP
            for g in range(len(acc) // 2):
                both = x_ref[g, pl.ds(pl.multiple_of(at, 2 * GROUP), 2 * GROUP), :].astype(jnp.float32)
                a = both[:GROUP] - first
                b = both[GROUP:] - second
                acc[2 * g] = acc[2 * g] + a * a
                acc[2 * g + 1] = acc[2 * g + 1] + b * b
        return tuple(acc)

    return lax.fori_loop(0, rows // unroll, step, carry)


def zero_carry(groups):
    return tuple(jnp.zeros((GROUP, LANES), jnp.float32) for _ in range(2 * groups))


def store_carry(o_ref, acc):
    for g in range(len(acc) // 2):
        o_ref[pl.ds(g * GROUP, GROUP), :] = acc[2 * g] + acc[2 * g + 1]


def load_body(chunks, x_hbm, v_ref, x_ref, o_ref, sems):
    groups, total, _ = x_ref.shape
    rows = total // chunks

    def copy(c):
        window = pl.ds(pl.multiple_of(c * rows, 2 * GROUP), rows)
        return pltpu.make_async_copy(x_hbm.at[:, window, :], x_ref.at[:, window, :], sems.at[c])

    for c in range(chunks):
        copy(c).start()
    acc = zero_carry(groups)
    per = rows // GROUP
    for c in range(chunks):
        copy(c).wait()
        acc = square_rows(x_ref, c * per, v_ref, c * per, per, acc, per)
    store_carry(o_ref, acc)


def square_body(offsets, x_ref, v_ref, o_ref):
    offs = offsets()
    pieces = len(offs)
    groups = x_ref.shape[0]
    rows = v_ref.shape[0] // pieces
    acc = zero_carry(groups)
    for j in range(pieces):
        acc = square_rows(x_ref, pl.multiple_of(offs[j], BLOCK), v_ref, j * rows, rows, acc, rows)
    store_carry(o_ref, acc)


def weigh_body(offsets, relative, step_at, devices, workers, root_total, radius_ref, x_ref, v_ref, s_ref, out_ref, o_ref):
    offs = offsets()
    pieces = len(offs)
    groups = x_ref.shape[0]
    own = groups * GROUP
    rows = o_ref.shape[0] // pieces
    depth = BLOCK * GROUP
    corner = lax.broadcasted_iota(jnp.int32, (own, own), 0) == lax.broadcasted_iota(jnp.int32, (own, own), 1)
    outside = jnp.sum(jnp.where(corner, out_ref[step_at:step_at + 1, :], 0.0), axis=1, keepdims=True)
    squared = jnp.sum(s_ref[...], axis=1, keepdims=True) + outside
    factor = jnp.minimum(jnp.float32(1.0), radius_ref[step_at] * root_total / jnp.sqrt(squared))
    keep = jnp.float32(1.0 / devices) - jnp.sum(factor, axis=0, keepdims=True) / jnp.float32(workers)
    factor = factor / jnp.float32(workers)
    lane = lax.broadcasted_iota(jnp.int32, (GROUP, depth), 1)
    sub = lax.broadcasted_iota(jnp.int32, (GROUP, depth), 0)
    block = lax.broadcasted_iota(jnp.int32, (BLOCK, depth), 0)
    place = lax.broadcasted_iota(jnp.int32, (BLOCK, depth), 1)
    weights = []
    for g in range(groups):
        one = jnp.where(lane % GROUP == sub, factor[g * GROUP:(g + 1) * GROUP], 0.0)
        one = jnp.sum(one, axis=0, keepdims=True)
        full = jnp.where(place // GROUP == block, one, 0.0)
        high = full.astype(jnp.bfloat16)
        low = (full - high.astype(jnp.float32)).astype(jnp.bfloat16)
        weights.append(jnp.concatenate([high, low], axis=0))
    for j in range(pieces):
        base = pl.multiple_of(offs[j], BLOCK)

        def step(i, _):
            at = base + i * 2 * BLOCK
            total = None
            for g in range(groups):
                left = x_ref[g, pl.ds(pl.multiple_of(at * GROUP, depth), depth), :]
                right = x_ref[g, pl.ds(pl.multiple_of(at * GROUP + depth, depth), depth), :]
                part = jnp.dot(weights[g], jnp.concatenate([left, right], axis=1), preferred_element_type=jnp.float32)
                total = part if total is None else total + part
            total = total[:BLOCK] + total[BLOCK:]
            v_at = (j * rows if relative else base) + i * 2 * BLOCK
            o_at = j * rows + i * 2 * BLOCK
            for h in range(2):
                old = v_ref[pl.ds(pl.multiple_of(v_at + h * BLOCK, BLOCK), BLOCK), :]
                o_ref[pl.ds(pl.multiple_of(o_at + h * BLOCK, BLOCK), BLOCK), :] = keep * old + total[:, h * LANES:(h + 1) * LANES]
            return 0

        lax.fori_loop(0, rows // (2 * BLOCK), step, 0, unroll=min(4, rows // (2 * BLOCK)))


VM = pl.BlockSpec(memory_space=pltpu.VMEM)
SM = pl.BlockSpec(memory_space=pltpu.SMEM)
PARAMS = pltpu.CompilerParams(vmem_limit_bytes=VMEM_LIMIT)


def shards(gradients, center, outside_sq, radius):
    workers, size = gradients.shape
    iters = outside_sq.shape[0]
    devices = lax.axis_size("worker")
    parts = lax.axis_size("mp")
    levels = bits_of(devices)
    root_total = float(size * parts) ** 0.5
    groups = workers // GROUP
    rows = size // LANES
    x = gradients.reshape(groups, GROUP, rows, LANES).transpose(0, 2, 1, 3).reshape(groups, rows * GROUP, LANES)
    center = center.reshape(rows, LANES)

    orders = [list(range(levels)), [1, 0] + list(range(2, levels))]
    streams = len(orders)
    height = rows // streams
    count = 1 << (levels - 2)
    piece = height >> (levels - 1)

    def turns(s):
        position = lax.axis_index("worker")
        odd = lax.axis_index("mp") & 1
        out = []
        for k in range(levels):
            ways = [(position >> orders[(s + c) % 2][k]) & 1 for c in range(2)]
            out.append(ways[0] + odd * (ways[1] - ways[0]))
        return out

    def offsets(s, first):
        bit = turns(s)
        out = []
        for j in range(count):
            off = s * height + (bit[0] ^ first) * (height >> 1)
            for k in range(1, levels - 1):
                r = (j >> (levels - 2 - k)) & 1
                off = off + (bit[k] ^ r) * (height >> (k + 1))
            out.append(off)
        return out

    partial_shape = jax.ShapeDtypeStruct((workers, LANES), jnp.float32)

    chunks = 16
    x, partial = pl.pallas_call(
        functools.partial(load_body, chunks),
        out_shape=(jax.ShapeDtypeStruct(x.shape, x.dtype), partial_shape),
        in_specs=[pl.BlockSpec(memory_space=pltpu.HBM), VM],
        out_specs=(VM, VM),
        scratch_shapes=[pltpu.SemaphoreType.DMA((chunks,))],
        compiler_params=PARAMS,
        name="load",
    )(pltpu.with_memory_space_constraint(x, pltpu.HBM), center)

    def squares(s, first, value):
        return pl.pallas_call(
            functools.partial(square_body, functools.partial(offsets, s, first)),
            out_shape=partial_shape, in_specs=[VM, VM], out_specs=VM, compiler_params=PARAMS, name="squares",
        )(x, value)

    def weigh(s, first, value, relative, step, squared):
        return pl.pallas_call(
            functools.partial(weigh_body, functools.partial(offsets, s, first), relative, step, devices, workers * devices, root_total),
            out_shape=jax.ShapeDtypeStruct((height >> 1, LANES), jnp.float32),
            in_specs=[SM, VM, VM, VM, VM], out_specs=VM, compiler_params=PARAMS, name="weigh",
        )(radius, x, value, squared, outside_sq)

    def exchange(value, s, k):
        pairs = []
        for w in range(devices):
            for m in range(parts):
                other = w ^ (1 << orders[(s + m) % 2][k])
                pairs.append((w * parts + m, other * parts + m))
        return lax.ppermute(value, ("worker", "mp"), pairs)

    value = None
    for t in range(iters):
        for b in range(bits_of(parts)):
            partial = partial + lax.ppermute(partial, "mp", swap(parts, b))
        squared = partial
        hold = []
        for s in range(streams):
            sent = weigh(s, 1, center if t == 0 else value[s][1], t > 0, t, squared)
            hold.append(exchange(sent, s, 0))
        for s in range(streams):
            hold[s] = hold[s] + weigh(s, 0, center if t == 0 else value[s][0], t > 0, t, squared)
        for k in range(1, levels - 1):
            for s in range(streams):
                half = hold[s].shape[0] // 2
                hold[s] = hold[s][:half] + exchange(hold[s][half:], s, k)
        for s in range(streams):
            hold[s] = hold[s] + exchange(hold[s], s, levels - 1)
        for k in reversed(range(1, levels - 1)):
            for s in range(streams):
                hold[s] = jnp.concatenate([hold[s], exchange(hold[s], s, k)], axis=0)
        value = [[hold[s], exchange(hold[s], s, 0)] for s in range(streams)]
        if t + 1 < iters:
            partial = None
            for first in range(2):
                for s in range(streams):
                    one = squares(s, first, value[s][first])
                    partial = one if partial is None else partial + one

    norms = jnp.sqrt(jnp.sum(squared, axis=1) + outside_sq[iters - 1])
    final = []
    for s in range(streams):
        tree = [value[s][f][j * piece:(j + 1) * piece] for f in range(2) for j in range(count)]
        for k in reversed(range(levels - 1)):
            turned = turns(s)[k] == 1
            tree = [
                jnp.where(turned, jnp.concatenate([b, a]), jnp.concatenate([a, b]))
                for a, b in zip(tree[0::2], tree[1::2])
            ]
        final.append(tree[0])
    return jnp.concatenate(final).reshape(size), norms


def solution(mesh):
    placed = (P("worker", "mp"), P("mp"), P(None, "worker"), P())
    return jax.shard_map(
        shards, mesh=mesh, in_specs=placed, out_specs=(P("mp"), P("worker")), check_vma=False
    )
```

```python
import functools

import jax
import jax.numpy as jnp
from jax import lax
from jax.experimental import pallas as pl
from jax.experimental.pallas import tpu as pltpu
from jax.sharding import PartitionSpec as P

LANES = 128
GROUP = 8
BLOCK = 32
VMEM_LIMIT = 24 << 20
SHARES = (1, 1, 1, 1)
FULL = 1


def bits_of(size):
    count = size.bit_length() - 1
    assert 1 << count == size
    return count


def swap(size, bit):
    return [(i, i ^ (1 << bit)) for i in range(size)]


def square_rows(x_ref, x_row, v_ref, v_row, rows, carry):
    unroll = 16

    def step(i, acc):
        acc = list(acc)
        for r in range(0, unroll, 2):
            row = v_row + i * unroll + r
            first = v_ref[pl.ds(row, 1), :]
            second = v_ref[pl.ds(row + 1, 1), :]
            at = (x_row + i * unroll + r) * GROUP
            for g in range(len(acc) // 2):
                both = x_ref[g, pl.ds(pl.multiple_of(at, 2 * GROUP), 2 * GROUP), :].astype(jnp.float32)
                a = both[:GROUP] - first
                b = both[GROUP:] - second
                acc[2 * g] = acc[2 * g] + a * a
                acc[2 * g + 1] = acc[2 * g + 1] + b * b
        return tuple(acc)

    return lax.fori_loop(0, rows // unroll, step, carry)


def zero_carry(groups):
    return tuple(jnp.zeros((GROUP, LANES), jnp.float32) for _ in range(2 * groups))


def store_carry(o_ref, acc, extra_ref, step):
    for g in range(len(acc) // 2):
        total = acc[2 * g] + acc[2 * g + 1]
        if step is not None:
            total = total + extra_ref[step, g * GROUP:(g + 1) * GROUP, :]
        o_ref[g * GROUP:(g + 1) * GROUP, :] = total


def load_body(chunks, parts, x_hbm, v_hbm, out_ref, x_ref, v_ref, o_ref, extra_ref, sems):
    groups, total, _ = x_ref.shape
    rows = total // chunks
    per = rows // GROUP
    own = groups * GROUP

    def copies(c):
        window = pl.ds(c * rows, rows)
        part = pl.ds(c * per, per)
        return (
            pltpu.make_async_copy(x_hbm.at[:, window, :], x_ref.at[:, window, :], sems.at[0, c]),
            pltpu.make_async_copy(v_hbm.at[part, :], v_ref.at[part, :], sems.at[1, c]),
        )

    for c in range(chunks):
        for copy in copies(c):
            copy.start()
    corner = lax.broadcasted_iota(jnp.int32, (own, own), 0) == lax.broadcasted_iota(jnp.int32, (own, own), 1)
    lane = lax.broadcasted_iota(jnp.int32, (own, LANES), 1)
    for t in range(extra_ref.shape[0]):
        column = jnp.sum(jnp.where(corner, out_ref[t:t + 1, :], 0.0), axis=1, keepdims=True)
        extra_ref[t] = jnp.where(lane == 0, column / jnp.float32(parts), 0.0)
    acc = zero_carry(groups)
    for c in range(chunks):
        for copy in copies(c):
            copy.wait()
        acc = square_rows(x_ref, c * per, v_ref, c * per, per, acc)
    store_carry(o_ref, acc, extra_ref, 0)


def square_body(offsets, extra, x_ref, v_ref, *refs):
    offs = offsets()
    groups = x_ref.shape[0]
    rows = v_ref.shape[0] // len(offs)
    acc = zero_carry(groups)
    for j, off in enumerate(offs):
        acc = square_rows(x_ref, pl.multiple_of(off, BLOCK), v_ref, j * rows, rows, acc)
    store_carry(refs[-1], acc, refs[0], extra)


def build_weights(root, workers, devices, groups, s_ref, w_ref, k_ref):
    depth = BLOCK * GROUP
    ones = jnp.ones((GROUP, LANES), jnp.bfloat16)
    block = lax.broadcasted_iota(jnp.int32, (BLOCK, depth), 0)
    place = lax.broadcasted_iota(jnp.int32, (BLOCK, depth), 1)
    total = None
    for g in range(groups):
        one = s_ref[g * GROUP:(g + 1) * GROUP, :]
        two = jnp.concatenate([one, one], axis=0)
        high = two.astype(jnp.bfloat16)
        low = (two - high.astype(jnp.float32)).astype(jnp.bfloat16)
        squared = None
        for half in (high, low):
            tall = jnp.concatenate([half] * (BLOCK // 2), axis=0)
            part = lax.dot_general(ones, tall, (((1,), (1,)), ((), ())), preferred_element_type=jnp.float32)
            squared = part if squared is None else squared + part
        factor = jnp.minimum(jnp.float32(1.0), root / jnp.sqrt(squared))
        total = factor if total is None else total + factor
        factor = factor[0:1] / jnp.float32(workers)
        high = factor.astype(jnp.bfloat16).astype(jnp.float32)
        low = factor - high
        for h, half in enumerate((high, low)):
            w_ref[g, h * BLOCK:(h + 1) * BLOCK, :] = jnp.where(place // GROUP == block, half, 0.0).astype(jnp.bfloat16)
    share = jnp.sum(total, axis=1, keepdims=True) / jnp.float32(BLOCK * workers)
    k_ref[...] = jnp.broadcast_to(jnp.float32(1.0 / devices) - share, k_ref.shape)


def weigh_rows(offs, relative, x_ref, v_ref, w_ref, k_ref, o_ref):
    groups = x_ref.shape[0]
    rows = o_ref.shape[0] // len(offs)
    depth = BLOCK * GROUP
    keep = k_ref[0:1, :]
    steps = rows // (2 * BLOCK)
    for j, off in enumerate(offs):
        base = pl.multiple_of(off, BLOCK)

        def step(i, _):
            at = base + i * 2 * BLOCK
            total = None
            for g in range(groups):
                left = x_ref[g, pl.ds(pl.multiple_of(at * GROUP, depth), depth), :]
                right = x_ref[g, pl.ds(pl.multiple_of(at * GROUP + depth, depth), depth), :]
                part = jnp.dot(w_ref[g], jnp.concatenate([left, right], axis=1), preferred_element_type=jnp.float32)
                total = part if total is None else total + part
            total = total[:BLOCK] + total[BLOCK:]
            v_at = (j * rows if relative else base) + i * 2 * BLOCK
            o_at = j * rows + i * 2 * BLOCK
            for h in range(2):
                old = v_ref[pl.ds(pl.multiple_of(v_at + h * BLOCK, BLOCK), BLOCK), :]
                o_ref[pl.ds(pl.multiple_of(o_at + h * BLOCK, BLOCK), BLOCK), :] = keep * old + total[:, h * LANES:(h + 1) * LANES]
            return 0

        lax.fori_loop(0, steps, step, 0, unroll=min(4, steps))


def first_body(offsets, relative, step_at, devices, workers, root_total, radius_ref, x_ref, v_ref, s_ref, o_ref, w_ref, k_ref):
    build_weights(radius_ref[step_at] * root_total, workers, devices, x_ref.shape[0], s_ref, w_ref, k_ref)
    weigh_rows(offsets(), relative, x_ref, v_ref, w_ref, k_ref, o_ref)


def weigh_body(offsets, relative, x_ref, v_ref, w_ref, k_ref, o_ref):
    weigh_rows(offsets(), relative, x_ref, v_ref, w_ref, k_ref, o_ref)


VM = pl.BlockSpec(memory_space=pltpu.VMEM)
SM = pl.BlockSpec(memory_space=pltpu.SMEM)
PARAMS = pltpu.CompilerParams(vmem_limit_bytes=VMEM_LIMIT)


def shards(gradients, center, outside_sq, radius):
    workers, size = gradients.shape
    iters = outside_sq.shape[0]
    devices = lax.axis_size("worker")
    parts = lax.axis_size("mp")
    levels = bits_of(devices)
    root_total = float(size * parts) ** 0.5
    groups = workers // GROUP
    rows = size // LANES
    x = gradients.reshape(groups, GROUP, rows, LANES).transpose(0, 2, 1, 3).reshape(groups, rows * GROUP, LANES)
    center = center.reshape(rows, LANES)

    ways = [list(range(levels)), [1, 0] + list(range(2, levels))]
    streams = len(SHARES)
    split = levels - FULL
    count = 1 << (split - 1)
    heights = [rows * share // sum(SHARES) for share in SHARES]
    starts = [sum(heights[:s]) for s in range(streams)]

    def order(s, c):
        return ways[(s + c) % 2]

    def turns(s):
        position = lax.axis_index("worker")
        odd = lax.axis_index("mp") & 1
        out = []
        for k in range(split):
            even, uneven = [(position >> order(s, c)[k]) & 1 for c in range(2)]
            out.append(even + odd * (uneven - even))
        return out

    def offsets(s, first):
        bit = turns(s)
        out = []
        for j in range(count):
            off = starts[s] + (bit[0] ^ first) * (heights[s] >> 1)
            for k in range(1, split):
                r = (j >> (split - 1 - k)) & 1
                off = off + (bit[k] ^ r) * (heights[s] >> (k + 1))
            out.append(off)
        return out

    partial_shape = jax.ShapeDtypeStruct((workers, LANES), jnp.float32)

    chunks = 16
    x, center, partial, extra = pl.pallas_call(
        functools.partial(load_body, chunks, parts),
        out_shape=(
            jax.ShapeDtypeStruct(x.shape, x.dtype),
            jax.ShapeDtypeStruct(center.shape, center.dtype),
            partial_shape,
            jax.ShapeDtypeStruct((iters, workers, LANES), jnp.float32),
        ),
        in_specs=[pl.BlockSpec(memory_space=pltpu.HBM), pl.BlockSpec(memory_space=pltpu.HBM), VM],
        out_specs=(VM, VM, VM, VM),
        scratch_shapes=[pltpu.SemaphoreType.DMA((2, chunks))],
        compiler_params=PARAMS,
        name="load",
    )(pltpu.with_memory_space_constraint(x, pltpu.HBM), pltpu.with_memory_space_constraint(center, pltpu.HBM), outside_sq)

    def squares(s, first, value, step):
        more = [] if step is None else [extra]
        return pl.pallas_call(
            functools.partial(square_body, functools.partial(offsets, s, first), step),
            out_shape=partial_shape, in_specs=[VM] * (2 + len(more)), out_specs=VM, compiler_params=PARAMS, name="squares",
        )(x, value, *more)

    weight_shape = jax.ShapeDtypeStruct((groups, 2 * BLOCK, BLOCK * GROUP), jnp.bfloat16)
    keep_shape = jax.ShapeDtypeStruct((GROUP, LANES), jnp.float32)

    def half_shape(s):
        return jax.ShapeDtypeStruct((heights[s] >> 1, LANES), jnp.float32)

    def weigh_first(s, first, value, relative, step, squared):
        body = functools.partial(
            first_body, functools.partial(offsets, s, first), relative, step, devices, workers * devices, root_total
        )
        return pl.pallas_call(
            body, out_shape=(half_shape(s), weight_shape, keep_shape),
            in_specs=[SM, VM, VM, VM], out_specs=(VM, VM, VM), compiler_params=PARAMS, name="first",
        )(radius, x, value, squared)

    def weigh(s, first, value, relative, weights, keep):
        return pl.pallas_call(
            functools.partial(weigh_body, functools.partial(offsets, s, first), relative),
            out_shape=half_shape(s), in_specs=[VM, VM, VM, VM], out_specs=VM, compiler_params=PARAMS, name="weigh",
        )(x, value, weights, keep)

    def exchange(value, s, k):
        pairs = []
        for w in range(devices):
            for m in range(parts):
                other = w ^ (1 << order(s, m % 2)[k])
                pairs.append((w * parts + m, other * parts + m))
        return lax.ppermute(value, ("worker", "mp"), pairs)

    value = None
    for t in range(iters):
        for b in range(bits_of(parts)):
            partial = partial + lax.ppermute(partial, "mp", swap(parts, b))
        squared = partial
        hold = []
        relative = t > 0
        for s in range(streams):
            source = value[s][1] if relative else center
            if s == 0:
                sent, weights, keep = weigh_first(s, 1, source, relative, t, squared)
            else:
                sent = weigh(s, 1, source, relative, weights, keep)
            hold.append(exchange(sent, s, 0))
        for s in range(streams):
            source = value[s][0] if relative else center
            hold[s] = hold[s] + weigh(s, 0, source, relative, weights, keep)
        for k in range(1, split):
            for s in range(streams):
                half = hold[s].shape[0] // 2
                hold[s] = hold[s][:half] + exchange(hold[s][half:], s, k)
        for k in range(split, levels):
            for s in range(streams):
                hold[s] = hold[s] + exchange(hold[s], s, k)
        for k in reversed(range(1, split)):
            for s in range(streams):
                hold[s] = jnp.concatenate([hold[s], exchange(hold[s], s, k)], axis=0)
        value = [[hold[s], exchange(hold[s], s, 0)] for s in range(streams)]
        if t + 1 < iters:
            partial = None
            for first in range(2):
                for s in range(streams):
                    one = squares(s, first, value[s][first], t + 1 if partial is None else None)
                    partial = one if partial is None else partial + one

    norms = jnp.sqrt(jnp.sum(squared, axis=1))
    final = []
    for s in range(streams):
        piece = heights[s] >> split
        tree = [value[s][f][j * piece:(j + 1) * piece] for f in range(2) for j in range(count)]
        for k in reversed(range(split)):
            turned = turns(s)[k] == 1
            tree = [
                jnp.where(turned, jnp.concatenate([b, a]), jnp.concatenate([a, b]))
                for a, b in zip(tree[0::2], tree[1::2])
            ]
        final.append(tree[0])
    return jnp.concatenate(final).reshape(size), norms


def solution(mesh):
    placed = (P("worker", "mp"), P("mp"), P(None, "worker"), P())
    return jax.shard_map(
        shards, mesh=mesh, in_specs=placed, out_specs=(P("mp"), P("worker")), check_vma=False
    )
```

```python
import functools

import jax
import jax.numpy as jnp
from jax import lax
from jax.experimental import pallas as pl
from jax.experimental.pallas import tpu as pltpu
from jax.sharding import PartitionSpec as P


LANES = 128
GROUP = 8
BLOCK = 32
VMEM_LIMIT = 24 << 20
SHARES = (1, 1, 1, 1)
FULL = 1


def bits_of(size):
    count = size.bit_length() - 1
    assert 1 << count == size
    return count


def square_rows(x_ref, x_row, v_ref, v_row, rows, carry):
    unroll = 16

    def step(i, acc):
        acc = list(acc)
        for r in range(0, unroll, 2):
            row = v_row + i * unroll + r
            first = v_ref[pl.ds(row, 1), :]
            second = v_ref[pl.ds(row + 1, 1), :]
            at = (x_row + i * unroll + r) * GROUP
            for g in range(len(acc) // 2):
                both = x_ref[g, pl.ds(pl.multiple_of(at, 2 * GROUP), 2 * GROUP), :].astype(jnp.float32)
                a = both[:GROUP] - first
                b = both[GROUP:] - second
                acc[2 * g] = acc[2 * g] + a * a
                acc[2 * g + 1] = acc[2 * g + 1] + b * b
        return tuple(acc)

    return lax.fori_loop(0, rows // unroll, step, carry)


def zero_carry(groups):
    return tuple(jnp.zeros((GROUP, LANES), jnp.float32) for _ in range(2 * groups))


def store_carry(o_ref, acc, extra_ref, step):
    for g in range(len(acc) // 2):
        total = acc[2 * g] + acc[2 * g + 1]
        if step is not None:
            total = total + extra_ref[step, g * GROUP:(g + 1) * GROUP, :]
        o_ref[g * GROUP:(g + 1) * GROUP, :] = total


def load_body(chunks, parts, x_hbm, v_hbm, out_hbm, x_ref, v_ref, o_ref, extra_ref, out_ref, sems, sem):
    groups, total, _ = x_ref.shape
    rows = total // chunks
    per = rows // GROUP
    own = groups * GROUP

    def copies(c):
        window = pl.ds(c * rows, rows)
        part = pl.ds(c * per, per)
        return (
            pltpu.make_async_copy(x_hbm.at[:, window, :], x_ref.at[:, window, :], sems.at[0, c]),
            pltpu.make_async_copy(v_hbm.at[part, :], v_ref.at[part, :], sems.at[1, c]),
        )

    small = pltpu.make_async_copy(out_hbm, out_ref, sem)
    small.start()
    for c in range(chunks):
        for copy in copies(c):
            copy.start()
    acc = zero_carry(groups)
    for c in range(chunks):
        for copy in copies(c):
            copy.wait()
        acc = square_rows(x_ref, c * per, v_ref, c * per, per, acc)
    small.wait()
    corner = lax.broadcasted_iota(jnp.int32, (own, own), 0) == lax.broadcasted_iota(jnp.int32, (own, own), 1)
    lane = lax.broadcasted_iota(jnp.int32, (own, LANES), 1)
    for t in range(extra_ref.shape[0]):
        column = jnp.sum(jnp.where(corner, out_ref[t:t + 1, :], 0.0), axis=1, keepdims=True)
        extra_ref[t] = jnp.where(lane == 0, column / jnp.float32(parts), 0.0)
    store_carry(o_ref, acc, extra_ref, 0)


def square_body(offsets, extra, x_ref, v_ref, *refs):
    offs = offsets()
    groups = x_ref.shape[0]
    rows = v_ref.shape[0] // len(offs)
    acc = zero_carry(groups)
    for j, off in enumerate(offs):
        acc = square_rows(x_ref, pl.multiple_of(off, BLOCK), v_ref, j * rows, rows, acc)
    store_carry(refs[-1], acc, refs[0], extra)


def build_weights(root, workers, devices, groups, s_ref, w_ref, k_ref):
    depth = BLOCK * GROUP
    ones = jnp.ones((GROUP, LANES), jnp.bfloat16)
    block = lax.broadcasted_iota(jnp.int32, (BLOCK, depth), 0)
    place = lax.broadcasted_iota(jnp.int32, (BLOCK, depth), 1)
    total = None
    for g in range(groups):
        one = s_ref[g * GROUP:(g + 1) * GROUP, :]
        two = jnp.concatenate([one, one], axis=0)
        high = two.astype(jnp.bfloat16)
        low = (two - high.astype(jnp.float32)).astype(jnp.bfloat16)
        squared = None
        for half in (high, low):
            tall = jnp.concatenate([half] * (BLOCK // 2), axis=0)
            part = lax.dot_general(ones, tall, (((1,), (1,)), ((), ())), preferred_element_type=jnp.float32)
            squared = part if squared is None else squared + part
        factor = jnp.minimum(jnp.float32(1.0), root / jnp.sqrt(squared))
        total = factor if total is None else total + factor
        factor = factor[0:1] / jnp.float32(workers)
        high = factor.astype(jnp.bfloat16).astype(jnp.float32)
        low = factor - high
        for h, half in enumerate((high, low)):
            w_ref[g, h * BLOCK:(h + 1) * BLOCK, :] = jnp.where(place // GROUP == block, half, 0.0).astype(jnp.bfloat16)
    share = jnp.sum(total, axis=1, keepdims=True) / jnp.float32(BLOCK * workers)
    k_ref[...] = jnp.broadcast_to(jnp.float32(1.0 / devices) - share, k_ref.shape)


def weigh_rows(offs, relative, x_ref, v_ref, w_ref, k_ref, o_ref):
    groups = x_ref.shape[0]
    rows = o_ref.shape[0] // len(offs)
    depth = BLOCK * GROUP
    keep = k_ref[0:1, :]
    steps = rows // (2 * BLOCK)
    for j, off in enumerate(offs):
        base = pl.multiple_of(off, BLOCK)

        def step(i, _):
            at = base + i * 2 * BLOCK
            total = None
            for g in range(groups):
                left = x_ref[g, pl.ds(pl.multiple_of(at * GROUP, depth), depth), :]
                right = x_ref[g, pl.ds(pl.multiple_of(at * GROUP + depth, depth), depth), :]
                part = jnp.dot(w_ref[g], jnp.concatenate([left, right], axis=1), preferred_element_type=jnp.float32)
                total = part if total is None else total + part
            total = total[:BLOCK] + total[BLOCK:]
            v_at = (j * rows if relative else base) + i * 2 * BLOCK
            o_at = j * rows + i * 2 * BLOCK
            for h in range(2):
                old = v_ref[pl.ds(pl.multiple_of(v_at + h * BLOCK, BLOCK), BLOCK), :]
                o_ref[pl.ds(pl.multiple_of(o_at + h * BLOCK, BLOCK), BLOCK), :] = keep * old + total[:, h * LANES:(h + 1) * LANES]
            return 0

        lax.fori_loop(0, steps, step, 0, unroll=min(4, steps))


def first_body(offsets, relative, step_at, devices, workers, root_total, radius_ref, x_ref, v_ref, s_ref, o_ref, w_ref, k_ref):
    build_weights(radius_ref[step_at] * root_total, workers, devices, x_ref.shape[0], s_ref, w_ref, k_ref)
    weigh_rows(offsets(), relative, x_ref, v_ref, w_ref, k_ref, o_ref)


def weigh_body(offsets, relative, x_ref, v_ref, w_ref, k_ref, o_ref):
    weigh_rows(offsets(), relative, x_ref, v_ref, w_ref, k_ref, o_ref)


VM = pl.BlockSpec(memory_space=pltpu.VMEM)
SM = pl.BlockSpec(memory_space=pltpu.SMEM)
PARAMS = pltpu.CompilerParams(vmem_limit_bytes=VMEM_LIMIT)


def shards(gradients, center, outside_sq, radius):
    workers, size = gradients.shape
    iters = outside_sq.shape[0]
    devices = lax.axis_size("worker")
    parts = lax.axis_size("mp")
    levels = bits_of(devices)
    root_total = float(size * parts) ** 0.5
    groups = workers // GROUP
    rows = size // LANES
    x = gradients.reshape(groups, GROUP, rows, LANES).transpose(0, 2, 1, 3).reshape(groups, rows * GROUP, LANES)
    center = center.reshape(rows, LANES)

    ways = [list(range(levels)), [1, 0] + list(range(2, levels))]
    streams = len(SHARES)
    split = levels - FULL
    count = 1 << (split - 1)
    heights = [rows * share // sum(SHARES) for share in SHARES]
    starts = [sum(heights[:s]) for s in range(streams)]

    def order(s, c):
        return ways[(s + c) % 2]

    def turns(s):
        position = lax.axis_index("worker")
        odd = lax.axis_index("mp") & 1
        out = []
        for k in range(split):
            even, uneven = [(position >> order(s, c)[k]) & 1 for c in range(2)]
            out.append(even + odd * (uneven - even))
        return out

    def offsets(s, first):
        bit = turns(s)
        out = []
        for j in range(count):
            off = starts[s] + (bit[0] ^ first) * (heights[s] >> 1)
            for k in range(1, split):
                r = (j >> (split - 1 - k)) & 1
                off = off + (bit[k] ^ r) * (heights[s] >> (k + 1))
            out.append(off)
        return out

    partial_shape = jax.ShapeDtypeStruct((workers, LANES), jnp.float32)

    chunks = 16
    x, center, partial, extra = pl.pallas_call(
        functools.partial(load_body, chunks, parts),
        out_shape=(
            jax.ShapeDtypeStruct(x.shape, x.dtype),
            jax.ShapeDtypeStruct(center.shape, center.dtype),
            partial_shape,
            jax.ShapeDtypeStruct((iters, workers, LANES), jnp.float32),
        ),
        in_specs=[pl.BlockSpec(memory_space=pltpu.HBM)] * 3,
        out_specs=(VM, VM, VM, VM),
        scratch_shapes=[
            pltpu.VMEM((iters, workers), jnp.float32), pltpu.SemaphoreType.DMA((2, chunks)), pltpu.SemaphoreType.DMA,
        ],
        compiler_params=PARAMS,
        name="load",
    )(*[pltpu.with_memory_space_constraint(a, pltpu.HBM) for a in (x, center, outside_sq)])

    def squares(s, first, value, step):
        more = [] if step is None else [extra]
        return pl.pallas_call(
            functools.partial(square_body, functools.partial(offsets, s, first), step),
            out_shape=partial_shape, in_specs=[VM] * (2 + len(more)), out_specs=VM, compiler_params=PARAMS, name="squares",
        )(x, value, *more)

    weight_shape = jax.ShapeDtypeStruct((groups, 2 * BLOCK, BLOCK * GROUP), jnp.bfloat16)
    keep_shape = jax.ShapeDtypeStruct((GROUP, LANES), jnp.float32)

    def half_shape(s):
        return jax.ShapeDtypeStruct((heights[s] >> 1, LANES), jnp.float32)

    def weigh_first(s, first, value, relative, step, squared):
        body = functools.partial(
            first_body, functools.partial(offsets, s, first), relative, step, devices, workers * devices, root_total
        )
        return pl.pallas_call(
            body, out_shape=(half_shape(s), weight_shape, keep_shape),
            in_specs=[SM, VM, VM, VM], out_specs=(VM, VM, VM), compiler_params=PARAMS, name="first",
        )(radius, x, value, squared)

    def weigh(s, first, value, relative, weights, keep):
        return pl.pallas_call(
            functools.partial(weigh_body, functools.partial(offsets, s, first), relative),
            out_shape=half_shape(s), in_specs=[VM, VM, VM, VM], out_specs=VM, compiler_params=PARAMS, name="weigh",
        )(x, value, weights, keep)

    def over_parts(one):
        for mask in [(1 << b) | 1 for b in reversed(range(1, bits_of(parts)))] + [1]:
            one = one + lax.ppermute(one, "mp", [(i, i ^ mask) for i in range(parts)])
        return one

    def exchange(value, s, k):
        pairs = []
        for w in range(devices):
            for m in range(parts):
                other = w ^ (1 << order(s, m % 2)[k])
                pairs.append((w * parts + m, other * parts + m))
        return lax.ppermute(value, ("worker", "mp"), pairs)

    value = None
    for t in range(iters):
        squared = over_parts(partial)
        hold = []
        relative = t > 0

        for s in range(streams):
            source = value[s][1] if relative else center
            if s == 0:
                sent, weights, keep = weigh_first(s, 1, source, relative, t, squared)
            else:
                sent = weigh(s, 1, source, relative, weights, keep)
            hold.append(exchange(sent, s, 0))
        for s in range(streams):
            source = value[s][0] if relative else center
            own = weigh(s, 0, source, relative, weights, keep)
            hold[s] = hold[s] + own
        for k in range(1, split):
            for s in range(streams):
                half = hold[s].shape[0] // 2
                other = exchange(hold[s][half:], s, k)
                hold[s] = hold[s][:half] + other
        for k in range(split, levels):
            for s in range(streams):
                other = exchange(hold[s], s, k)
                hold[s] = hold[s] + other
        for k in reversed(range(1, split)):
            for s in range(streams):
                other = exchange(hold[s], s, k)
                hold[s] = jnp.concatenate([hold[s], other], axis=0)
        value = []
        for s in range(streams):
            value.append([hold[s], exchange(hold[s], s, 0)])
        if t + 1 < iters:
            partial = None
            for first in range(2):
                for s in range(streams):
                    one = squares(s, first, value[s][first], t + 1 if partial is None else None)
                    partial = one if partial is None else partial + one

    norms = jnp.sqrt(jnp.sum(squared, axis=1))
    final = []
    for s in range(streams):
        piece = heights[s] >> split
        tree = [value[s][f][j * piece:(j + 1) * piece] for f in range(2) for j in range(count)]
        for k in reversed(range(split)):
            turned = turns(s)[k] == 1
            tree = [
                jnp.where(turned, jnp.concatenate([b, a]), jnp.concatenate([a, b]))
                for a, b in zip(tree[0::2], tree[1::2])
            ]
        final.append(tree[0])
    return jnp.concatenate(final).reshape(size), norms


def solution(mesh):
    placed = (P("worker", "mp"), P("mp"), P(None, "worker"), P())

    return jax.shard_map(shards, mesh=mesh, in_specs=placed, out_specs=(P("mp"), P("worker")), check_vma=False)
```

```python
import functools

import jax
import jax.numpy as jnp
from jax import lax
from jax.experimental import pallas as pl
from jax.experimental.pallas import tpu as pltpu
from jax.sharding import PartitionSpec as P


LANES = 128
GROUP = 8
BLOCK = 32
VMEM_LIMIT = 24 << 20
SHARES = (1, 1)
SEND = ((3, 1, 2), (1, 2, 3))
BACK = ((3, 1, 2), (3, 1, 2))


def bits_of(size):
    count = size.bit_length() - 1
    assert 1 << count == size
    return count


def square_rows(x_ref, x_row, v_ref, v_row, rows, carry):
    unroll = min(64, rows)
    assert rows % unroll == 0 and unroll % 2 == 0

    def step(i, acc):
        acc = list(acc)
        for r in range(0, unroll, 2):
            row = v_row + i * unroll + r
            first = v_ref[pl.ds(row, 1), :]
            second = v_ref[pl.ds(row + 1, 1), :]
            at = (x_row + i * unroll + r) * GROUP
            for g in range(len(acc) // 2):
                both = x_ref[g, pl.ds(pl.multiple_of(at, 2 * GROUP), 2 * GROUP), :].astype(jnp.float32)
                a = both[:GROUP] - first
                b = both[GROUP:] - second
                acc[2 * g] = acc[2 * g] + a * a
                acc[2 * g + 1] = acc[2 * g + 1] + b * b
        return tuple(acc)

    return lax.fori_loop(0, rows // unroll, step, carry)


def zero_carry(groups):
    return tuple(jnp.zeros((GROUP, LANES), jnp.float32) for _ in range(2 * groups))


def store_carry(o_ref, acc, extra_ref, step):
    for g in range(len(acc) // 2):
        total = acc[2 * g] + acc[2 * g + 1]
        if step is not None:
            total = total + extra_ref[step, g * GROUP:(g + 1) * GROUP, :]
        o_ref[g * GROUP:(g + 1) * GROUP, :] = total


def load_body(chunks, parts, x_hbm, v_hbm, out_hbm, x_ref, v_ref, o_ref, extra_ref, out_ref, sems, sem):
    groups, total, _ = x_ref.shape
    rows = total // chunks
    per = rows // GROUP
    own = groups * GROUP

    def copies(c):
        window = pl.ds(c * rows, rows)
        part = pl.ds(c * per, per)
        return (
            pltpu.make_async_copy(x_hbm.at[:, window, :], x_ref.at[:, window, :], sems.at[0, c]),
            pltpu.make_async_copy(v_hbm.at[part, :], v_ref.at[part, :], sems.at[1, c]),
        )

    small = pltpu.make_async_copy(out_hbm, out_ref, sem)
    small.start()
    for c in range(chunks):
        for copy in copies(c):
            copy.start()
    acc = zero_carry(groups)
    for c in range(chunks):
        for copy in copies(c):
            copy.wait()
        acc = square_rows(x_ref, c * per, v_ref, c * per, per, acc)
    small.wait()
    corner = lax.broadcasted_iota(jnp.int32, (own, own), 0) == lax.broadcasted_iota(jnp.int32, (own, own), 1)
    lane = lax.broadcasted_iota(jnp.int32, (own, LANES), 1)
    for t in range(extra_ref.shape[0]):
        column = jnp.sum(jnp.where(corner, out_ref[t:t + 1, :], 0.0), axis=1, keepdims=True)
        extra_ref[t] = jnp.where(lane == 0, column / jnp.float32(parts), 0.0)
    store_carry(o_ref, acc, extra_ref, 0)


def square_body(offset, extra, x_ref, v_ref, *refs):
    acc = zero_carry(x_ref.shape[0])
    acc = square_rows(x_ref, pl.multiple_of(offset(), BLOCK), v_ref, 0, v_ref.shape[0], acc)
    store_carry(refs[-1], acc, refs[0], extra)


def build_weights(root, workers, devices, groups, s_ref, w_ref, k_ref):
    depth = BLOCK * GROUP
    ones = jnp.ones((GROUP, LANES), jnp.bfloat16)
    block = lax.broadcasted_iota(jnp.int32, (BLOCK, depth), 0)
    place = lax.broadcasted_iota(jnp.int32, (BLOCK, depth), 1)
    total = None
    for g in range(groups):
        one = s_ref[g * GROUP:(g + 1) * GROUP, :]
        two = jnp.concatenate([one, one], axis=0)
        high = two.astype(jnp.bfloat16)
        low = (two - high.astype(jnp.float32)).astype(jnp.bfloat16)
        squared = None
        for half in (high, low):
            tall = jnp.concatenate([half] * (BLOCK // 2), axis=0)
            part = lax.dot_general(ones, tall, (((1,), (1,)), ((), ())), preferred_element_type=jnp.float32)
            squared = part if squared is None else squared + part
        factor = jnp.minimum(jnp.float32(1.0), root / jnp.sqrt(squared))
        total = factor if total is None else total + factor
        factor = factor[0:1] / jnp.float32(workers)
        high = factor.astype(jnp.bfloat16).astype(jnp.float32)
        low = factor - high
        for h, half in enumerate((high, low)):
            w_ref[g, h * BLOCK:(h + 1) * BLOCK, :] = jnp.where(place // GROUP == block, half, 0.0).astype(jnp.bfloat16)
    share = jnp.sum(total, axis=1, keepdims=True) / jnp.float32(BLOCK * workers)
    k_ref[...] = jnp.broadcast_to(jnp.float32(1.0 / devices) - share, k_ref.shape)


def weigh_rows(off, relative, x_ref, v_ref, w_ref, k_ref, o_ref):
    groups = x_ref.shape[0]
    depth = BLOCK * GROUP
    keep = k_ref[0:1, :]
    steps = o_ref.shape[0] // (2 * BLOCK)
    base = pl.multiple_of(off, BLOCK)

    def step(i, _):
        at = base + i * 2 * BLOCK
        total = None
        for g in range(groups):
            left = x_ref[g, pl.ds(pl.multiple_of(at * GROUP, depth), depth), :]
            right = x_ref[g, pl.ds(pl.multiple_of(at * GROUP + depth, depth), depth), :]
            part = jnp.dot(w_ref[g], jnp.concatenate([left, right], axis=1), preferred_element_type=jnp.float32)
            total = part if total is None else total + part
        total = total[:BLOCK] + total[BLOCK:]
        o_at = i * 2 * BLOCK
        v_at = o_at if relative else at
        for h in range(2):
            old = v_ref[pl.ds(pl.multiple_of(v_at + h * BLOCK, BLOCK), BLOCK), :]
            o_ref[pl.ds(pl.multiple_of(o_at + h * BLOCK, BLOCK), BLOCK), :] = keep * old + total[:, h * LANES:(h + 1) * LANES]
        return 0

    lax.fori_loop(0, steps, step, 0, unroll=min(4, steps))


def first_body(offset, relative, step_at, devices, workers, root_total, radius_ref, x_ref, v_ref, s_ref, o_ref, w_ref, k_ref):
    build_weights(radius_ref[step_at] * root_total, workers, devices, x_ref.shape[0], s_ref, w_ref, k_ref)
    weigh_rows(offset(), relative, x_ref, v_ref, w_ref, k_ref, o_ref)


def weigh_body(offset, relative, x_ref, v_ref, w_ref, k_ref, o_ref):
    weigh_rows(offset(), relative, x_ref, v_ref, w_ref, k_ref, o_ref)


VM = pl.BlockSpec(memory_space=pltpu.VMEM)
SM = pl.BlockSpec(memory_space=pltpu.SMEM)
PARAMS = pltpu.CompilerParams(vmem_limit_bytes=VMEM_LIMIT)


def shards(gradients, center, outside_sq, radius):
    workers, size = gradients.shape
    iters = outside_sq.shape[0]
    devices = lax.axis_size("worker")
    parts = lax.axis_size("mp")
    levels = bits_of(devices)
    root_total = float(size * parts) ** 0.5
    groups = workers // GROUP
    rows = size // LANES
    x = gradients.reshape(groups, GROUP, rows, LANES).transpose(0, 2, 1, 3).reshape(groups, rows * GROUP, LANES)
    center = center.reshape(rows, LANES)

    streams = len(SHARES)
    heights = [rows * share // sum(SHARES) for share in SHARES]
    starts = [sum(heights[:s]) for s in range(streams)]

    def offset(s, r):
        return starts[s] + ((lax.axis_index("worker") & 3) ^ r) * (heights[s] >> 2)

    partial_shape = jax.ShapeDtypeStruct((workers, LANES), jnp.float32)

    chunks = 16
    x, center, partial, extra = pl.pallas_call(
        functools.partial(load_body, chunks, parts),
        out_shape=(
            jax.ShapeDtypeStruct(x.shape, x.dtype),
            jax.ShapeDtypeStruct(center.shape, center.dtype),
            partial_shape,
            jax.ShapeDtypeStruct((iters, workers, LANES), jnp.float32),
        ),
        in_specs=[pl.BlockSpec(memory_space=pltpu.HBM)] * 3,
        out_specs=(VM, VM, VM, VM),
        scratch_shapes=[
            pltpu.VMEM((iters, workers), jnp.float32), pltpu.SemaphoreType.DMA((2, chunks)), pltpu.SemaphoreType.DMA,
        ],
        compiler_params=PARAMS,
        name="load",
    )(*[pltpu.with_memory_space_constraint(a, pltpu.HBM) for a in (x, center, outside_sq)])

    def squares(s, r, value, step):
        more = [] if step is None else [extra]
        return pl.pallas_call(
            functools.partial(square_body, functools.partial(offset, s, r), step),
            out_shape=partial_shape, in_specs=[VM] * (2 + len(more)), out_specs=VM, compiler_params=PARAMS, name="squares",
        )(x, value, *more)

    weight_shape = jax.ShapeDtypeStruct((groups, 2 * BLOCK, BLOCK * GROUP), jnp.bfloat16)
    keep_shape = jax.ShapeDtypeStruct((GROUP, LANES), jnp.float32)

    def quarter_shape(s):
        return jax.ShapeDtypeStruct((heights[s] >> 2, LANES), jnp.float32)

    def weigh_first(s, r, value, relative, step, squared):
        body = functools.partial(
            first_body, functools.partial(offset, s, r), relative, step, devices, workers * devices, root_total
        )
        return pl.pallas_call(
            body, out_shape=(quarter_shape(s), weight_shape, keep_shape),
            in_specs=[SM, VM, VM, VM], out_specs=(VM, VM, VM), compiler_params=PARAMS, name="first",
        )(radius, x, value, squared)

    def weigh(s, r, value, relative, weights, keep):
        return pl.pallas_call(
            functools.partial(weigh_body, functools.partial(offset, s, r), relative),
            out_shape=quarter_shape(s), in_specs=[VM, VM, VM, VM], out_specs=VM, compiler_params=PARAMS, name="weigh",
        )(x, value, weights, keep)

    def over_parts(one):
        for mask in [(1 << b) | 1 for b in reversed(range(1, bits_of(parts)))] + [1]:
            one = one + lax.ppermute(one, "mp", [(i, i ^ mask) for i in range(parts)])
        return one

    def exchange(value, mask):
        return lax.ppermute(value, "worker", [(w, w ^ mask) for w in range(devices)])

    value = None
    for t in range(iters):
        squared = over_parts(partial)
        relative = t > 0
        got = [[None] * 4 for _ in range(streams)]
        weights = None
        for s in range(streams):
            for r in SEND[s]:
                source = value[s][r] if relative else center
                if weights is None:
                    sent, weights, keep = weigh_first(s, r, source, relative, t, squared)
                else:
                    sent = weigh(s, r, source, relative, weights, keep)
                got[s][r] = exchange(sent, r)
        hold = []
        for s in range(streams):
            own = weigh(s, 0, value[s][0] if relative else center, relative, weights, keep)
            hold.append((own + got[s][1]) + (got[s][2] + got[s][3]))
        for k in range(1, levels - 1):
            for s in range(streams):
                other = exchange(hold[s], 2 << k)
                hold[s] = hold[s] + other
        value = [[hold[s]] + [None] * 3 for s in range(streams)]
        for s in range(streams):
            for r in BACK[s]:
                value[s][r] = exchange(hold[s], r)
        if t + 1 < iters:
            partial = None
            for i in range(4):
                for s in range(streams):
                    r = ((0,) + BACK[s])[i]
                    one = squares(s, r, value[s][r], t + 1 if partial is None else None)
                    partial = one if partial is None else partial + one

    norms = jnp.sqrt(jnp.sum(squared, axis=1))
    final = []
    for s in range(streams):
        tree = value[s]
        for k in range(2):
            turned = (lax.axis_index("worker") >> k) & 1 == 1
            tree = [
                jnp.where(turned, jnp.concatenate([b, a]), jnp.concatenate([a, b]))
                for a, b in zip(tree[0::2], tree[1::2])
            ]
        final.append(tree[0])
    return jnp.concatenate(final).reshape(size), norms


def solution(mesh):
    placed = (P("worker", "mp"), P("mp"), P(None, "worker"), P())

    return jax.shard_map(shards, mesh=mesh, in_specs=placed, out_specs=(P("mp"), P("worker")), check_vma=False)
```

```python
import functools

import jax
import jax.numpy as jnp
from jax import lax
from jax.experimental import pallas as pl
from jax.experimental.pallas import tpu as pltpu
from jax.sharding import PartitionSpec as P


LANES = 128
GROUP = 8
BLOCK = 32
VMEM_LIMIT = 24 << 20
SHARES = (1, 1)
SEND = ((3, 1, 2), (1, 2, 3))
BACK = ((3, 1, 2), (3, 1, 2))


def bits_of(size):
    count = size.bit_length() - 1
    assert 1 << count == size
    return count


def square_rows(x_ref, x_row, v_ref, v_row, rows, carry):
    unroll = min(64, rows)
    assert rows % unroll == 0 and unroll % 2 == 0

    def step(i, acc):
        acc = list(acc)
        for r in range(0, unroll, 2):
            row = v_row + i * unroll + r
            first = v_ref[pl.ds(row, 1), :]
            second = v_ref[pl.ds(row + 1, 1), :]
            at = (x_row + i * unroll + r) * GROUP
            for g in range(len(acc) // 2):
                both = x_ref[g, pl.ds(pl.multiple_of(at, 2 * GROUP), 2 * GROUP), :].astype(jnp.float32)
                a = both[:GROUP] - first
                b = both[GROUP:] - second
                acc[2 * g] = acc[2 * g] + a * a
                acc[2 * g + 1] = acc[2 * g + 1] + b * b
        return tuple(acc)

    return lax.fori_loop(0, rows // unroll, step, carry)


def zero_carry(groups):
    return tuple(jnp.zeros((GROUP, LANES), jnp.float32) for _ in range(2 * groups))


def store_carry(o_ref, acc, extra_ref, step):
    for g in range(len(acc) // 2):
        total = acc[2 * g] + acc[2 * g + 1]
        if step is not None:
            total = total + extra_ref[step, g * GROUP:(g + 1) * GROUP, :]
        o_ref[g * GROUP:(g + 1) * GROUP, :] = total


def load_body(chunks, parts, x_hbm, v_hbm, out_hbm, x_ref, v_ref, o_ref, extra_ref, out_ref, sems, sem):
    groups, total, _ = x_ref.shape
    rows = total // chunks
    per = rows // GROUP
    own = groups * GROUP

    def copies(c):
        window = pl.ds(c * rows, rows)
        part = pl.ds(c * per, per)
        return (
            pltpu.make_async_copy(x_hbm.at[:, window, :], x_ref.at[:, window, :], sems.at[0, c]),
            pltpu.make_async_copy(v_hbm.at[part, :], v_ref.at[part, :], sems.at[1, c]),
        )

    small = pltpu.make_async_copy(out_hbm, out_ref, sem)
    small.start()
    for c in range(chunks):
        for copy in copies(c):
            copy.start()
    acc = zero_carry(groups)
    for c in range(chunks):
        for copy in copies(c):
            copy.wait()
        acc = square_rows(x_ref, c * per, v_ref, c * per, per, acc)
    small.wait()
    corner = lax.broadcasted_iota(jnp.int32, (own, own), 0) == lax.broadcasted_iota(jnp.int32, (own, own), 1)
    lane = lax.broadcasted_iota(jnp.int32, (own, LANES), 1)
    for t in range(extra_ref.shape[0]):
        column = jnp.sum(jnp.where(corner, out_ref[t:t + 1, :], 0.0), axis=1, keepdims=True)
        extra_ref[t] = jnp.where(lane == 0, column / jnp.float32(parts), 0.0)
    store_carry(o_ref, acc, extra_ref, 0)


def square_body(offset, extra, x_ref, v_ref, *refs):
    acc = zero_carry(x_ref.shape[0])
    acc = square_rows(x_ref, pl.multiple_of(offset(), BLOCK), v_ref, 0, v_ref.shape[0], acc)
    store_carry(refs[-1], acc, refs[0], extra)


def build_weights(root, workers, devices, groups, s_ref, w_ref, k_ref):
    depth = BLOCK * GROUP
    block = lax.broadcasted_iota(jnp.int32, (BLOCK, depth), 0)
    place = lax.broadcasted_iota(jnp.int32, (BLOCK, depth), 1)
    lane = lax.broadcasted_iota(jnp.int32, (GROUP, depth), 1)
    sub = lax.broadcasted_iota(jnp.int32, (GROUP, depth), 0)
    total = None
    for g in range(groups):
        squared = jnp.sum(s_ref[g * GROUP:(g + 1) * GROUP, :], axis=1, keepdims=True)
        factor = jnp.minimum(jnp.float32(1.0), root / jnp.sqrt(squared))
        total = factor if total is None else total + factor
        factor = jnp.where(lane % GROUP == sub, factor, 0.0)
        factor = jnp.sum(factor, axis=0, keepdims=True) / jnp.float32(workers)
        high = factor.astype(jnp.bfloat16).astype(jnp.float32)
        low = factor - high
        for h, half in enumerate((high, low)):
            w_ref[g, h * BLOCK:(h + 1) * BLOCK, :] = jnp.where(place // GROUP == block, half, 0.0).astype(jnp.bfloat16)
    share = jnp.sum(total, axis=0, keepdims=True) / jnp.float32(workers)
    k_ref[...] = jnp.broadcast_to(jnp.float32(1.0 / devices) - share, k_ref.shape)


def weigh_rows(off, relative, x_ref, v_ref, w_ref, k_ref, o_ref):
    groups = x_ref.shape[0]
    depth = BLOCK * GROUP
    keep = k_ref[0:1, :]
    steps = o_ref.shape[0] // (2 * BLOCK)
    base = pl.multiple_of(off, BLOCK)

    def step(i, _):
        at = base + i * 2 * BLOCK
        total = None
        for g in range(groups):
            left = x_ref[g, pl.ds(pl.multiple_of(at * GROUP, depth), depth), :]
            right = x_ref[g, pl.ds(pl.multiple_of(at * GROUP + depth, depth), depth), :]
            part = jnp.dot(w_ref[g], jnp.concatenate([left, right], axis=1), preferred_element_type=jnp.float32)
            total = part if total is None else total + part
        total = total[:BLOCK] + total[BLOCK:]
        o_at = i * 2 * BLOCK
        v_at = o_at if relative else at
        for h in range(2):
            old = v_ref[pl.ds(pl.multiple_of(v_at + h * BLOCK, BLOCK), BLOCK), :]
            o_ref[pl.ds(pl.multiple_of(o_at + h * BLOCK, BLOCK), BLOCK), :] = keep * old + total[:, h * LANES:(h + 1) * LANES]
        return 0

    lax.fori_loop(0, steps, step, 0, unroll=min(4, steps))


def first_body(offset, relative, step_at, devices, workers, root_total, radius_ref, x_ref, v_ref, s_ref, o_ref, w_ref, k_ref):
    build_weights(radius_ref[step_at] * root_total, workers, devices, x_ref.shape[0], s_ref, w_ref, k_ref)
    weigh_rows(offset(), relative, x_ref, v_ref, w_ref, k_ref, o_ref)


def weigh_body(offset, relative, x_ref, v_ref, w_ref, k_ref, o_ref):
    weigh_rows(offset(), relative, x_ref, v_ref, w_ref, k_ref, o_ref)


VM = pl.BlockSpec(memory_space=pltpu.VMEM)
SM = pl.BlockSpec(memory_space=pltpu.SMEM)
PARAMS = pltpu.CompilerParams(vmem_limit_bytes=VMEM_LIMIT)


def shards(gradients, center, outside_sq, radius):
    workers, size = gradients.shape
    iters = outside_sq.shape[0]
    devices = lax.axis_size("worker")
    parts = lax.axis_size("mp")
    levels = bits_of(devices)
    root_total = float(size * parts) ** 0.5
    groups = workers // GROUP
    rows = size // LANES
    x = gradients.reshape(groups, GROUP, rows, LANES).transpose(0, 2, 1, 3).reshape(groups, rows * GROUP, LANES)
    center = center.reshape(rows, LANES)

    streams = len(SHARES)
    heights = [rows * share // sum(SHARES) for share in SHARES]
    starts = [sum(heights[:s]) for s in range(streams)]

    def offset(s, r):
        return starts[s] + ((lax.axis_index("worker") & 3) ^ r) * (heights[s] >> 2)

    partial_shape = jax.ShapeDtypeStruct((workers, LANES), jnp.float32)

    chunks = 16
    x, center, partial, extra = pl.pallas_call(
        functools.partial(load_body, chunks, parts),
        out_shape=(
            jax.ShapeDtypeStruct(x.shape, x.dtype),
            jax.ShapeDtypeStruct(center.shape, center.dtype),
            partial_shape,
            jax.ShapeDtypeStruct((iters, workers, LANES), jnp.float32),
        ),
        in_specs=[pl.BlockSpec(memory_space=pltpu.HBM)] * 3,
        out_specs=(VM, VM, VM, VM),
        scratch_shapes=[
            pltpu.VMEM((iters, workers), jnp.float32), pltpu.SemaphoreType.DMA((2, chunks)), pltpu.SemaphoreType.DMA,
        ],
        compiler_params=PARAMS,
        name="load",
    )(*[pltpu.with_memory_space_constraint(a, pltpu.HBM) for a in (x, center, outside_sq)])

    def squares(s, r, value, step):
        more = [] if step is None else [extra]
        return pl.pallas_call(
            functools.partial(square_body, functools.partial(offset, s, r), step),
            out_shape=partial_shape, in_specs=[VM] * (2 + len(more)), out_specs=VM, compiler_params=PARAMS, name="squares",
        )(x, value, *more)

    weight_shape = jax.ShapeDtypeStruct((groups, 2 * BLOCK, BLOCK * GROUP), jnp.bfloat16)
    keep_shape = jax.ShapeDtypeStruct((GROUP, LANES), jnp.float32)

    def quarter_shape(s):
        return jax.ShapeDtypeStruct((heights[s] >> 2, LANES), jnp.float32)

    def weigh_first(s, r, value, relative, step, squared):
        body = functools.partial(
            first_body, functools.partial(offset, s, r), relative, step, devices, workers * devices, root_total
        )
        return pl.pallas_call(
            body, out_shape=(quarter_shape(s), weight_shape, keep_shape),
            in_specs=[SM, VM, VM, VM], out_specs=(VM, VM, VM), compiler_params=PARAMS, name="first",
        )(radius, x, value, squared)

    def weigh(s, r, value, relative, weights, keep):
        return pl.pallas_call(
            functools.partial(weigh_body, functools.partial(offset, s, r), relative),
            out_shape=quarter_shape(s), in_specs=[VM, VM, VM, VM], out_specs=VM, compiler_params=PARAMS, name="weigh",
        )(x, value, weights, keep)

    def over_parts(one):
        for mask in [(1 << b) | 1 for b in reversed(range(1, bits_of(parts)))] + [1]:
            one = one + lax.ppermute(one, "mp", [(i, i ^ mask) for i in range(parts)])
        return one

    def exchange(value, mask):
        return lax.ppermute(value, "worker", [(w, w ^ mask) for w in range(devices)])

    value = None
    for t in range(iters):
        squared = over_parts(partial)
        relative = t > 0
        got = [[None] * 4 for _ in range(streams)]
        weights = None
        for s in range(streams):
            for r in SEND[s]:
                source = value[s][r] if relative else center
                if weights is None:
                    sent, weights, keep = weigh_first(s, r, source, relative, t, squared)
                else:
                    sent = weigh(s, r, source, relative, weights, keep)
                got[s][r] = exchange(sent, r)
        hold = []
        for s in range(streams):
            own = weigh(s, 0, value[s][0] if relative else center, relative, weights, keep)
            hold.append((own + got[s][1]) + (got[s][2] + got[s][3]))
        for k in range(1, levels - 1):
            for s in range(streams):
                other = exchange(hold[s], 2 << k)
                hold[s] = hold[s] + other
        value = [[hold[s]] + [None] * 3 for s in range(streams)]
        for s in range(streams):
            for r in BACK[s]:
                value[s][r] = exchange(hold[s], r)
        if t + 1 < iters:
            partial = None
            for i in range(4):
                for s in range(streams):
                    r = ((0,) + BACK[s])[i]
                    one = squares(s, r, value[s][r], t + 1 if partial is None else None)
                    partial = one if partial is None else partial + one

    norms = jnp.sqrt(jnp.sum(squared, axis=1))
    final = []
    for s in range(streams):
        tree = value[s]
        for k in range(2):
            turned = (lax.axis_index("worker") >> k) & 1 == 1
            tree = [
                jnp.where(turned, jnp.concatenate([b, a]), jnp.concatenate([a, b]))
                for a, b in zip(tree[0::2], tree[1::2])
            ]
        final.append(tree[0])
    return jnp.concatenate(final).reshape(size), norms


def solution(mesh):
    placed = (P("worker", "mp"), P("mp"), P(None, "worker"), P())

    return jax.shard_map(shards, mesh=mesh, in_specs=placed, out_specs=(P("mp"), P("worker")), check_vma=False)
```
